32 devices in a mesh: ctx: 8 (over z, x), exp: 4 (over y, core).
Axes of the slice: x: 2, y: 2, z: 4, core: 2. Of those that a mesh axis runs over, the one named last changes fastest.
Arguments:
- hidden_states: bfloat16 [4096, 4096], P(('ctx', 'exp')), may hold values from -70 to 70
- upstream: bfloat16 [4096, 4096], P(('ctx', 'exp')), may hold values from -6 to 6
- norm_gain: float32 [4096], replicated, may hold values from 0.5 to 1.5
- router: bfloat16 [4096, 8], replicated, may hold values from -4 to 4
- expert_ids: int32 [4096, 8], P(('ctx', 'exp')), may hold values from 0 to 7, as said below
- w_gate: bfloat16 [8, 4096, 1536], P('ctx', None, 'exp'), may hold values from -0.09375 to 0.09375
- w_up: bfloat16 [8, 4096, 1536], P('ctx', None, 'exp'), may hold values from -0.09375 to 0.09375
- w_down: bfloat16 [8, 1536, 4096], P('ctx', 'exp'), may hold values from -0.15625 to 0.15625
Outputs:
- grad_input: bfloat16 [4096, 4096], P(('ctx', 'exp'))
The draws below stay inside these ranges and needn't reach their ends.
Inputs may be any that keep to these rules, and one draw needn't show every extreme that they name: `expert_ids`: A token's 8 entries differ. Among the rows of one device, no expert is named in column 0 by more than 24 rows, and in every device's rows one expert is named there by exactly 24.
All inputs are finite; a program needn't handle non-finite values.
Results may differ from the reference program's by a relative error of at most 0.012.
Values may be sent and summed in bfloat16 or wider, within the bound.
A program may use at most 128 MiB of HBM per device.

```python
import jax
import jax.numpy as jnp
from jax import lax

D = 4096
FF = 1536
TOPK = 8
TOK_DEV = 128
E = 8
TOKENS = 4096
CAP = 24
N_CTX = 8
N_EXP = 4


def draw_hidden_states(key, part):
    key_base, key_rows, key_cols = jax.random.split(key, 3)
    row_scale = jnp.exp(jax.random.uniform(key_rows, (TOKENS, 1), jnp.float32, 0.0, 0.693147))
    col_scale = jnp.exp(jax.random.uniform(key_cols, (1, D), jnp.float32, 0.0, 2.302585))
    base_values = jnp.clip(jax.random.normal(key_base, (TOKENS, D), jnp.float32), -3.5, 3.5)
    return (base_values * row_scale * col_scale).astype(jnp.bfloat16)


def draw_router(key, part):
    key_base, key_scale = jax.random.split(key, 2)
    weights = jnp.clip(jax.random.normal(key_base, (D, E), jnp.float32), -4.0, 4.0)
    scales = jnp.exp(jax.random.uniform(key_scale, (1, E), jnp.float32, -1.049822, -0.356675))
    values = weights * scales
    return jnp.clip(values * D ** (-0.5), -4.0, 4.0).astype(jnp.bfloat16)


def one_block(block_key):
    key_full, key_score, key_shuffle, key_other = jax.random.split(block_key, 4)
    slot_total = E * CAP
    slot_ids = jnp.arange(slot_total, dtype=jnp.int32)
    owner_expert = slot_ids // CAP
    full_expert = jax.random.randint(key_full, (), 0, E, dtype=jnp.int32)
    random_score = jax.random.randint(key_score, (slot_total,), 0, 1 << 19, dtype=jnp.int32)
    scores = jnp.where(owner_expert == full_expert, slot_ids - slot_total, random_score * slot_total + slot_ids)
    ranking = jnp.argsort(scores)
    picked = owner_expert[ranking[:TOK_DEV]]
    shuffle_score = jax.random.randint(key_shuffle, (TOK_DEV,), 0, 1 << 19, dtype=jnp.int32) * TOK_DEV + jnp.arange(TOK_DEV, dtype=jnp.int32)
    picked = picked[jnp.argsort(shuffle_score)]
    labels = jnp.arange(E, dtype=jnp.int32)
    other_score = jax.random.randint(key_other, (TOK_DEV, E), 0, 1 << 19, dtype=jnp.int32) * E + labels[None, :]
    other_score = jnp.where(labels[None, :] == picked[:, None], -1, other_score)
    ranked = jnp.argsort(other_score, axis=1)[:, :TOPK]
    return ranked.astype(jnp.int32)


def draw_expert_ids(key, part):
    block_keys = jax.random.split(key, TOKENS // TOK_DEV)
    return jax.vmap(one_block)(block_keys).reshape(TOKENS, TOPK)


def shard_levels(rng, extent, shards, low, high):
    def one(dim, parts):
        steps = jax.random.uniform(jax.random.fold_in(jax.random.fold_in(rng, 6), dim), (parts,), jnp.float32, low / len(shards), high / len(shards))
        return jnp.repeat(jnp.exp(steps), extent[dim] // parts).reshape((-1,) + (1,) * (len(extent) - dim - 1))

    factor_of = one(*shards[0])
    for cut in shards[1:]:
        factor_of = factor_of * one(*cut)
    return factor_of


def gaussian(own_key, shape, scale, limit, shards=(), kind=jnp.bfloat16):
    gain = shard_levels(own_key, shape, shards, -0.22, 0.18) if shards else 1.0
    entries = jax.random.normal(own_key, shape, jnp.float32) * scale * gain
    return jnp.minimum(jnp.maximum(entries, -limit), limit).astype(kind)


def setup_inputs(seed: int = 0) -> dict:
    arg_keys = jax.random.split(jax.random.key(seed), 9)
    return {
        "hidden_states": draw_hidden_states(jax.random.fold_in(arg_keys[8], 71), 0),
        "upstream": gaussian(arg_keys[1], (TOKENS, D), 1.0, 6.0, ((0, 32),)),
        "norm_gain": jnp.clip(1.0 + 0.1 * jax.random.normal(arg_keys[2], (D,), jnp.float32), 0.5, 1.5),
        "router": draw_router(jax.random.fold_in(arg_keys[8], 71), 0),
        "expert_ids": draw_expert_ids(jax.random.fold_in(arg_keys[8], 71), 0),
        "w_gate": gaussian(arg_keys[5], (E, D, FF), D ** -0.5, 0.09375, ((0, 8), (2, 4))),
        "w_up": gaussian(arg_keys[6], (E, D, FF), D ** -0.5, 0.09375, ((0, 8), (2, 4))),
        "w_down": gaussian(arg_keys[7], (E, FF, D), FF ** -0.5, 0.15625, ((0, 8), (1, 4))),
    }


EPSILON = 1e-06

def silu_parts(pre_value):
    sigmoid_value = jax.nn.sigmoid(pre_value)
    return (pre_value * sigmoid_value, sigmoid_value * (1.0 + pre_value * (1.0 - sigmoid_value)))

def reference(hidden_states, upstream, norm_gain, router, expert_ids, w_gate, w_up, w_down):
    widened = hidden_states.astype(jnp.float32)
    inverse = lax.rsqrt(lax.optimization_barrier(jnp.mean(widened * widened, axis=1, keepdims=True)) + EPSILON)
    normed = (widened * inverse * norm_gain).astype(jnp.bfloat16)
    logits = jnp.dot(normed, router, preferred_element_type=jnp.float32)
    probability = jax.nn.softmax(logits, axis=1)
    labels = jnp.arange(E, dtype=jnp.int32)
    chosen = (expert_ids[:, :, None] == labels).astype(jnp.float32)
    primary = chosen[:, 0, :]
    member = lax.optimization_barrier(jnp.sum(chosen, axis=1))
    top_prob = lax.optimization_barrier(jnp.sum(probability * primary, axis=1))
    route_mass = lax.optimization_barrier(jnp.sum(probability * member, axis=1))
    gate_value = top_prob / route_mass
    scaled_grad = (gate_value[:, None] * upstream.astype(jnp.float32)).astype(jnp.bfloat16)
    blocks = primary.reshape(N_CTX * N_EXP, TOK_DEV, E)
    before = jnp.cumsum(blocks, axis=1) - blocks
    slot_index = lax.optimization_barrier(jnp.sum(before * blocks, axis=2)).reshape(TOKENS).astype(jnp.int32)
    position = jnp.arange(TOKENS, dtype=jnp.int32)
    block_id = position // TOK_DEV
    row_index = block_id % N_EXP * (N_CTX * CAP) + block_id // N_EXP * CAP + slot_index
    token_of = jnp.full((E, N_EXP * N_CTX * CAP), TOKENS, jnp.int32).at[expert_ids[:, 0], row_index].set(position)
    shard_width = FF // N_EXP
    pad_row = jnp.zeros((1, D), jnp.bfloat16)
    normed_pad = jnp.concatenate([normed, pad_row], axis=0)
    grad_pad = jnp.concatenate([scaled_grad, pad_row], axis=0)

    def per_expert(totals, member_array):
        out_tokens, back_tokens = totals
        gate_block, up_block, down_block, token_rows = member_array
        expert_rows = normed_pad[token_rows]
        grad_rows = grad_pad[token_rows]
        row_count = expert_rows.shape[0]
        pre_gate = jnp.dot(expert_rows, gate_block, preferred_element_type=jnp.float32)
        pre_up = jnp.dot(expert_rows, up_block, preferred_element_type=jnp.float32)
        activated, act_slope = silu_parts(pre_gate)
        hidden = (activated * pre_up).astype(jnp.bfloat16)
        partials = jnp.einsum('rsf,sfd->srd', hidden.reshape(row_count, N_EXP, shard_width).astype(jnp.float32), down_block.reshape(N_EXP, shard_width, D).astype(jnp.float32))
        partials = lax.optimization_barrier(partials.astype(jnp.bfloat16)).astype(jnp.float32)
        expert_out = lax.optimization_barrier(jnp.sum(partials, axis=0)).astype(jnp.bfloat16)
        hidden_grad = lax.dot_general(grad_rows, down_block, (((1,), (1,)), ((), ())), preferred_element_type=jnp.float32)
        grad_pre_gate = (hidden_grad * pre_up * act_slope).astype(jnp.bfloat16)
        grad_pre_up = (hidden_grad * activated).astype(jnp.bfloat16)
        grad_partials = jnp.einsum('rsf,dsf->srd', grad_pre_gate.reshape(row_count, N_EXP, shard_width).astype(jnp.float32), gate_block.reshape(D, N_EXP, shard_width).astype(jnp.float32))
        grad_partials = grad_partials + jnp.einsum('rsf,dsf->srd', grad_pre_up.reshape(row_count, N_EXP, shard_width).astype(jnp.float32), up_block.reshape(D, N_EXP, shard_width).astype(jnp.float32))
        grad_partials = lax.optimization_barrier(grad_partials.astype(jnp.bfloat16)).astype(jnp.float32)
        expert_grad = lax.optimization_barrier(jnp.sum(grad_partials, axis=0)).astype(jnp.bfloat16)
        return ((out_tokens.at[token_rows].set(expert_out), back_tokens.at[token_rows].set(expert_grad)), None)
    start_value = jnp.zeros((TOKENS + 1, D), jnp.bfloat16)
    finals, unused = lax.scan(per_expert, (start_value, start_value), (w_gate, w_up, w_down, token_of))
    expert_out = finals[0][:TOKENS].astype(jnp.float32)
    expert_grad = finals[1][:TOKENS].astype(jnp.float32)
    gate_grad = lax.optimization_barrier(jnp.sum(upstream.astype(jnp.float32) * expert_out, axis=1))
    prob_grad = gate_grad[:, None] * (primary / route_mass[:, None] - (top_prob / (route_mass * route_mass))[:, None] * member)
    logit_grad = probability * (prob_grad - lax.optimization_barrier(jnp.sum(probability * prob_grad, axis=1, keepdims=True)))
    normed_grad = expert_grad + jnp.dot(logit_grad, router.astype(jnp.float32).T, precision=lax.Precision.HIGHEST)
    scaled = normed_grad * norm_gain
    grad_input = inverse * scaled - widened * inverse ** 3 * lax.optimization_barrier(jnp.sum(scaled * widened, axis=1, keepdims=True)) / D
    return grad_input.astype(jnp.bfloat16)
```

```python
import functools

import jax
import jax.numpy as jnp
from jax import lax
from jax.experimental import pallas as pl
from jax.experimental.pallas import tpu as pltpu
from jax.sharding import PartitionSpec as P

EPSILON = 1e-06
F32 = jnp.float32
BF16 = jnp.bfloat16
LANES = 128


def pick(rows_of, total, values):
    hot = (rows_of[None, :] == jnp.arange(total, dtype=jnp.int32)[:, None]).astype(BF16)
    return jnp.dot(hot, values, preferred_element_type=F32).astype(BF16)


def expert_math(normed_rows, up_rows, gate_block, up_block, down_block):
    pre_gate = jnp.dot(normed_rows, gate_block, preferred_element_type=F32)
    pre_up = jnp.dot(normed_rows, up_block, preferred_element_type=F32)
    raw_grad = lax.dot_general(
        up_rows, down_block, (((1,), (1,)), ((), ())), preferred_element_type=F32
    )
    sig = jax.nn.sigmoid(pre_gate)
    act = pre_gate * sig
    slope = sig * (1.0 + pre_gate * (1.0 - sig))
    hidden = (act * pre_up).astype(BF16).astype(F32)
    dots = jnp.sum(hidden * raw_grad, axis=1)
    grad_gate = (raw_grad * pre_up * slope).astype(BF16)
    grad_up = (raw_grad * act).astype(BF16)
    back = lax.dot_general(
        grad_gate, gate_block, (((1,), (1,)), ((), ())), preferred_element_type=F32
    ) + lax.dot_general(grad_up, up_block, (((1,), (1,)), ((), ())), preferred_element_type=F32)
    return back, dots


def exchange_collective(slots_normed, slots_up, gate_block, up_block, down_block):
    experts, capacity, width = slots_normed.shape

    def dispatch(shaped):
        moved = lax.all_to_all(shaped, "ctx", split_axis=0, concat_axis=0, tiled=True)
        return lax.all_gather(
            moved.reshape(experts * capacity, width), "exp", axis=0, tiled=True
        )

    back, dots = expert_math(
        dispatch(slots_normed), dispatch(slots_up), gate_block, up_block, down_block
    )
    summed = lax.psum_scatter(back.astype(BF16), "exp", scatter_dimension=0, tiled=True)
    dot_sum = lax.psum_scatter(dots, "exp", scatter_dimension=0, tiled=True)
    returned = lax.all_to_all(
        summed.reshape(experts, capacity, width), "ctx", split_axis=0, concat_axis=0, tiled=True
    )
    dot_back = lax.all_to_all(
        dot_sum.reshape(experts, capacity), "ctx", split_axis=0, concat_axis=0, tiled=True
    )
    return returned.reshape(experts * capacity, width), dot_back.reshape(experts * capacity)


def exclusive_or(left, right, count):
    total, bit = 0, 1
    while bit < count:
        total = total + bit * lax.rem(lax.div(left, bit) + lax.div(right, bit), 2)
        bit *= 2
    return total


SEND, ACROSS, RELAY, FORWARD, SLOPES, BACK, SUM, FINISH, WEIGHTS, DOTS, TOTALS, PICK, PROBS = range(13)
SCHEDULE = (
    176, 16, 178, 2, 8, 17, 180, 4, 182, 192, 128, 18, 3, 5, 9, 32, 33, 19,
    48, 49, 34, 10, 24, 64, 80, 81, 35, 6, 11, 7, 25, 50, 40, 51, 20, 66,
    82, 41, 21, 56, 12, 57, 72, 88, 26, 36, 89, 37, 98, 52, 53, 27, 68, 84,
    13, 42, 85, 22, 23, 83, 43, 58, 14, 59, 74, 90, 28, 38, 39, 29, 91, 15,
    55, 54, 44, 105, 104, 70, 86, 30, 45, 114, 60, 106, 107, 87, 120, 61, 76, 31,
    92, 121, 122, 93, 123, 46, 108, 103, 47, 102, 109, 62, 63, 99, 78, 144, 94, 124,
    119, 101, 110, 160, 125, 118, 95, 115, 100, 111, 126, 117, 127, 97, 116, 96, 113, 112,
)


def scheduled(step):
    at, inner = lax.div(step, 3), lax.rem(step, 3)
    word = jnp.int32(0)
    for place in range(0, len(SCHEDULE), 3):
        packed = sum(code * 256**i for i, code in enumerate(SCHEDULE[place : place + 3]))
        word = jnp.where(at == place // 3, jnp.int32(packed), word)
    word = jnp.where(
        inner == 0, word, jnp.where(inner == 1, lax.div(word, 256), lax.div(word, 65536))
    )
    return lax.rem(word, 256)


def exchange_body(
    count, capacity, hidden_hbm, upstream_hbm, gain_hbm, router_hbm, ids_hbm,
    gate_hbm, up_hbm, down_hbm, out_hbm,
    hidden, pair, gain, router, ids, inverse, routed, stats, turned, scaled, result, send, landing,
    both, down, rows, acc, grads, part, mate_in, mid, cross_in, done,
    dots, dots_in, dots_sum, dots_back, dots_all, total,
    weight_sem, local_sem, out_sem, send_sem, recv_sem, tiny_send, tiny_recv,
):
    tokens, width = hidden.shape
    half = width // 2
    quarter = width // 4
    units = down.shape[0]
    tall = -(-capacity // 16) * 16
    skip = tall - capacity
    ctx = lax.axis_index("ctx")
    exp = lax.axis_index("exp")
    row, core = lax.div(exp, 2), lax.rem(exp, 2)
    mate = row * 2 + (1 - core)
    cross = (1 - row) * 2 + core
    diagonal = (1 - row) * 2 + (1 - core)
    peers = (mate, cross, diagonal)

    def remote(src, dst, send, recv, device):
        return pltpu.make_async_remote_copy(
            src_ref=src, dst_ref=dst, send_sem=send, recv_sem=recv,
            device_id=device, device_id_type=pl.DeviceIdType.MESH,
        )

    def piece(kind, src, dst, c, device):
        return remote(src, dst, send_sem.at[kind, c], recv_sem.at[kind, c], device)

    def partner(k):
        return exclusive_or(ctx, k, count)

    def side(h):
        return pl.ds(pl.multiple_of(h * half, half), half)

    def direct(k, h):
        return piece(
            0, send.at[k, :, side(h)], rows.at[k, exp, :, side(h)], 2 * k + h,
            (partner(k), exp),
        )

    def to_mate(k, h):
        own = rows.at[k, exp, :, side(h)]
        return piece(1, own, own, 2 * k + h, (ctx, mate))

    def to_cross(k, h):
        own = rows.at[k, exp, :, side(h)]
        return piece(2, own, own, 2 * k + h, (ctx, cross))

    def relay(k, h):
        own = rows.at[k, cross, :, side(h)]
        return piece(3, own, own, 2 * k + h, (ctx, mate))

    def part_to_mate(c):
        return piece(4, part.at[c, 1 - core], mate_in.at[c], c, (ctx, mate))

    def sum_to_cross(c):
        return piece(5, mid.at[c], cross_in.at[c], c, (ctx, cross))

    def give_back(k, h):
        return piece(
            6, done.at[2 * k + h], landing.at[h, ctx], 2 * k + h, (partner(k), exp)
        )

    def dots_to(q):
        return remote(dots, dots_in.at[q], tiny_send.at[q], tiny_recv.at[q], (ctx, peers[q]))

    def totals_to(k):
        return remote(
            dots_sum, dots_back.at[k], tiny_send.at[2 + k], tiny_recv.at[2 + k],
            (partner(k), exp),
        )

    weights = [
        pltpu.make_async_copy(gate_hbm.at[0], both.at[:, pl.ds(0, units)], weight_sem.at[0]),
        pltpu.make_async_copy(up_hbm.at[0], both.at[:, pl.ds(units, units)], weight_sem.at[1]),
        pltpu.make_async_copy(down_hbm.at[0], down, weight_sem.at[2]),
    ]
    loads = [
        pltpu.make_async_copy(ids_hbm, ids, local_sem.at[0]),
        pltpu.make_async_copy(gain_hbm, gain, local_sem.at[1]),
        pltpu.make_async_copy(hidden_hbm, hidden, local_sem.at[2]),
        pltpu.make_async_copy(upstream_hbm, pair.at[pl.ds(tokens, tokens)], local_sem.at[3]),
        pltpu.make_async_copy(router_hbm, router, local_sem.at[4]),
    ]
    for copy in loads:
        copy.start()
    for copy in weights:
        copy.start()

    barrier = pltpu.get_barrier_semaphore()

    @pl.loop(1, count)
    def _(k):
        pl.semaphore_signal(
            barrier, inc=1, device_id=(partner(k), exp), device_id_type=pl.DeviceIdType.MESH
        )

    for other in peers:
        pl.semaphore_signal(
            barrier, inc=1, device_id=(ctx, other), device_id_type=pl.DeviceIdType.MESH
        )
    dots[...] = jnp.zeros_like(dots)
    loads[0].wait()
    experts = lax.broadcasted_iota(jnp.int32, (count, tokens), 0)
    first = ids[pl.ds(0, 1), :]
    primary = (first == experts).astype(F32)
    earlier = (
        lax.broadcasted_iota(jnp.int32, (tokens, tokens), 0)
        < lax.broadcasted_iota(jnp.int32, (tokens, tokens), 1)
    ).astype(BF16)
    before = jnp.dot(primary.astype(BF16), earlier, preferred_element_type=F32)
    slot = jnp.sum(before * primary, axis=0, keepdims=True).astype(jnp.int32)
    routed[pl.ds(0, 1), :] = slot

    loads[1].wait()
    loads[2].wait()

    @pl.loop(0, tokens // 16)
    def _(i):
        some = pl.ds(pl.multiple_of(i * 16, 16), 16)
        wide = hidden[some, :].astype(F32)
        scale = lax.rsqrt(jnp.mean(wide * wide, axis=1, keepdims=True) + EPSILON)
        inverse[some, :] = jnp.broadcast_to(scale, (16, LANES))
        pair[some, :] = (wide * scale * gain[...]).astype(BF16)

    loads[3].wait()

    def pick_rows(k):
        inner = lax.broadcasted_iota(jnp.int32, (2 * capacity, 2 * tokens), 0)
        token = lax.broadcasted_iota(jnp.int32, (2 * capacity, 2 * tokens), 1)
        place = jnp.where(
            ids[pl.ds(0, 1), :] == partner(k), routed[pl.ds(0, 1), :], -2 * capacity
        )
        wanted = jnp.concatenate([place, place + capacity], axis=1)
        upper = (token >= tokens) == (inner >= capacity)
        return jnp.logical_and(wanted == inner, upper).astype(F32)

    def pick(k):
        hot = jnp.concatenate([pick_rows(k), pick_rows(k + 4)], axis=0).astype(BF16)

        @pl.loop(0, 4)
        def _(j):
            columns = pl.ds(pl.multiple_of(j * quarter, quarter), quarter)
            found = jnp.dot(hot, pair[:, columns], preferred_element_type=F32).astype(BF16)

            @pl.when(k == 0)
            def _():
                rows[0, exp, :, columns] = found[: 2 * capacity]

            @pl.when(k > 0)
            def _():
                send[k, :, columns] = found[: 2 * capacity]

            send[k + 4, :, columns] = found[2 * capacity :]

    def shares():
        ids_all = ids[...]
        labels = lax.broadcasted_iota(jnp.int32, (count, tokens), 0)
        logits = lax.dot_general(
            router[...], pair[pl.ds(0, tokens), :], (((1,), (1,)), ((), ())),
            preferred_element_type=F32,
        )
        raised = jnp.exp(logits - jnp.max(logits, axis=0, keepdims=True))
        probability = raised / jnp.sum(raised, axis=0, keepdims=True)
        primary = (ids_all[:1] == labels).astype(F32)
        member = jnp.zeros((count, tokens), F32)
        for one in range(ids.shape[0]):
            member = member + (ids_all[one : one + 1] == labels).astype(F32)
        top_prob = jnp.sum(probability * primary, axis=0, keepdims=True)
        route_mass = jnp.sum(probability * member, axis=0, keepdims=True)
        return probability, primary, member, top_prob, route_mass

    pl.semaphore_wait(barrier, count + 2)

    @pl.loop(0, len(SCHEDULE))
    def _(step):
        code = scheduled(step)
        kind = lax.div(code, 16)
        c = lax.rem(code, 16)
        k = lax.div(c, 2)
        h = lax.rem(c, 2)

        @pl.when(kind == SEND)
        def _():
            direct(k, h).start()

        @pl.when(jnp.logical_and(kind == ACROSS, k > 0))
        def _():
            direct(k, h).wait_recv()

        @pl.when(kind == ACROSS)
        def _():
            to_cross(k, h).start()
            to_mate(k, h).start()

        @pl.when(kind == RELAY)
        def _():
            to_cross(k, h).wait_recv()
            relay(k, h).start()

        @pl.when(kind == PICK)
        def _():
            pick(k)

        @pl.when(kind == PROBS)
        def _():
            loads[4].wait()
            probability, primary, member, top_prob, route_mass = shares()
            place = ids[pl.ds(0, 1), :] * (2 * capacity) + routed[pl.ds(0, 1), :]
            stats[pl.ds(0, 8), :] = probability
            stats[pl.ds(8, 8), :] = primary / route_mass - (
                top_prob / (route_mass * route_mass)
            ) * member
            lines = jnp.concatenate(
                [
                    jnp.broadcast_to(top_prob / route_mass, (8, tokens)),
                    jnp.broadcast_to(place.astype(F32), (8, tokens)),
                    jnp.zeros((LANES - 16, tokens), F32),
                ],
                axis=0,
            )
            turned[...] = lines.T

        @pl.when(kind == WEIGHTS)
        def _():
            for copy in weights:
                copy.wait()
            acc[...] = jnp.zeros_like(acc)

        @pl.when(kind == FORWARD)
        def _():
            to_mate(k, h).wait_recv()
            relay(k, h).wait_recv()
            columns = side(h)
            acc[k, :, pl.ds(0, 2 * units)] += jnp.dot(
                rows[k, :, pl.ds(0, tall), columns].reshape(4 * tall, half),
                both[columns, :],
                preferred_element_type=F32,
            )
            acc[k, :, pl.ds(2 * units, units)] += lax.dot_general(
                rows[k, :, pl.ds(2 * capacity - tall, tall), columns].reshape(4 * tall, half),
                down[:, columns],
                (((1,), (1,)), ((), ())),
                preferred_element_type=F32,
            )

        @pl.when(kind == SLOPES)
        def _():
            pre_gate = acc[k, :, pl.ds(0, units)].reshape(4, tall, units)[:, :capacity]
            pre_up = acc[k, :, pl.ds(units, units)].reshape(4, tall, units)[:, :capacity]
            raw_grad = acc[k, :, pl.ds(2 * units, units)].reshape(4, tall, units)[:, skip:]
            sig = jax.nn.sigmoid(pre_gate)
            act = pre_gate * sig
            slope = sig * (1.0 + pre_gate * (1.0 - sig))
            hidden = (act * pre_up).astype(BF16).astype(F32)
            terms = (hidden * raw_grad).reshape(4 * capacity, units)
            high = terms.astype(BF16)
            low = (terms - high.astype(F32)).astype(BF16)
            ones = jnp.ones((8, units), BF16)
            lined = lax.dot_general(
                ones, high, (((1,), (1,)), ((), ())), preferred_element_type=F32
            ) + lax.dot_general(ones, low, (((1,), (1,)), ((), ())), preferred_element_type=F32)
            dots[pl.ds(k, 1), pl.ds(0, 4 * capacity)] = lined[:1]
            grads[k, :, pl.ds(0, units)] = (
                (raw_grad * pre_up * slope).reshape(4 * capacity, units).astype(BF16)
            )
            grads[k, :, pl.ds(units, units)] = (
                (raw_grad * act).reshape(4 * capacity, units).astype(BF16)
            )

        @pl.when(kind == BACK)
        def _():
            sides = []
            for side_index in range(2):
                start = pl.multiple_of(side_index * half + h * quarter, quarter)
                product = lax.dot_general(
                    grads[k],
                    both[pl.ds(start, quarter), :],
                    (((1,), (1,)), ((), ())),
                    preferred_element_type=F32,
                )
                sides.append(product.reshape(4, capacity, quarter))
            value = jnp.concatenate(sides, axis=1).astype(BF16)
            for one in range(4):
                part[c, one % 2, one // 2] = value[one]
            part_to_mate(c).start()

        @pl.when(kind == SUM)
        def _():
            part_to_mate(c).wait_recv()
            total = part[c, core, 1 - row].astype(F32) + mate_in[c, 1 - row].astype(F32)
            mid[c] = total.astype(BF16)
            sum_to_cross(c).start()

        @pl.when(kind == FINISH)
        def _():
            sum_to_cross(c).wait_recv()
            total = part[c, core, row].astype(F32) + mate_in[c, row].astype(F32)
            total = (total + cross_in[c].astype(F32)).astype(BF16)

            @pl.when(k == 0)
            def _():
                landing[h, ctx] = total

            @pl.when(k > 0)
            def _():
                done[c] = total
                give_back(k, h).start()

        @pl.when(kind == DOTS)
        def _():
            for q in range(3):
                dots_to(q).start()

        @pl.when(kind == TOTALS)
        def _():
            for q in range(3):
                dots_to(q).wait_recv()
            dots_sum[...] = dots[...] + dots_in[0] + dots_in[1] + dots_in[2]

            @pl.loop(1, count)
            def _(k):
                totals_to(k).start()

    dots_all[pl.ds(ctx, 1), :] = dots_sum[:1]

    @pl.loop(1, count)
    def _(k):
        totals_to(k).wait()
        dots_all[pl.ds(partner(k), 1), :] = dots_back[k, pl.ds(k, 1), :]

    at = lax.broadcasted_iota(jnp.int32, (LANES, tokens), 0)
    here = (at == routed[pl.ds(0, 1), :] + exp * capacity).astype(BF16)
    gathered = jnp.zeros((count, tokens), F32)
    rest = dots_all[...]
    for _ in range(3):
        high = rest.astype(BF16)
        rest = rest - high.astype(F32)
        gathered = gathered + jnp.dot(high, here, preferred_element_type=F32)
    labels = lax.broadcasted_iota(jnp.int32, (count, tokens), 0)
    gate_grad = jnp.sum(
        jnp.where(ids[pl.ds(0, 1), :] == labels, gathered, 0.0), axis=0, keepdims=True
    )
    probability = stats[pl.ds(0, 8), :]
    prob_grad = gate_grad * stats[pl.ds(8, 8), :]
    logit_grad = probability * (
        prob_grad - jnp.sum(probability * prob_grad, axis=0, keepdims=True)
    )
    high = logit_grad.astype(BF16).astype(F32)
    middle = (logit_grad - high).astype(BF16).astype(F32)
    low = logit_grad - high - middle
    lines = jnp.concatenate(
        [high, middle, low, jnp.zeros((LANES - 24, tokens), F32)], axis=0
    )
    logit_lines = lines.T.astype(BF16)
    gate = turned[:, pl.ds(0, 1)]
    place = turned[:, pl.ds(8, 1)].astype(jnp.int32)
    spot = lax.broadcasted_iota(jnp.int32, (tokens, 2 * capacity * count), 1)
    thrice = jnp.concatenate(
        [router[...].astype(F32)] * 3 + [jnp.zeros((LANES - 24, width), F32)], axis=0
    ).astype(BF16)
    total[...] = jnp.zeros_like(total)
    for h in range(2):

        @pl.loop(1, count)
        def _(k):
            give_back(k, h).wait_recv()

        found = landing[h].reshape(2 * capacity * count, quarter)
        for half_index in range(2):
            start = half_index * half + h * quarter
            columns = pl.ds(start, quarter)
            own = (place + half_index * capacity == spot).astype(BF16)
            back = gate * jnp.dot(own, found, preferred_element_type=F32)
            back = back + jnp.dot(
                logit_lines, thrice[:, start : start + quarter], preferred_element_type=F32
            )
            back = back * gain[:, columns]
            scaled[:, columns] = back
            along = back * hidden[:, columns].astype(F32)
            some = along[:, :LANES]
            for one in range(1, quarter // LANES):
                some = some + along[:, one * LANES : (one + 1) * LANES]
            total[...] += some

    def out_copy(i):
        some = pl.ds(pl.multiple_of(i * 32, 32), 32)
        return pltpu.make_async_copy(result.at[some], out_hbm.at[some], out_sem.at[i])

    @pl.loop(0, tokens // 32)
    def _(i):
        some = pl.ds(pl.multiple_of(i * 32, 32), 32)
        factor = inverse[some, pl.ds(0, 1)]
        weight = jnp.sum(total[some, :], axis=1, keepdims=True) * factor**3 / width
        result[some, :] = (
            factor * scaled[some, :] - hidden[some, :].astype(F32) * weight
        ).astype(BF16)
        out_copy(i).start()

    for q in range(3):
        dots_to(q).wait_send()

    @pl.loop(0, 2 * count)
    def _(c):
        k, h = lax.div(c, 2), lax.rem(c, 2)
        to_mate(k, h).wait_send()
        to_cross(k, h).wait_send()
        relay(k, h).wait_send()
        part_to_mate(c).wait_send()
        sum_to_cross(c).wait_send()

        @pl.when(k > 0)
        def _():
            direct(k, h).wait_send()
            give_back(k, h).wait_send()

    @pl.loop(0, tokens // 32)
    def _(i):
        out_copy(i).wait()


def exchange_kernel(capacity, hidden_states, upstream, gain, router, ids, w_gate, w_up, w_down):
    tokens, width = hidden_states.shape
    count, tall = router.shape[0], 2 * capacity
    units = w_down.shape[1]
    quarter = width // 4
    pieces = 2 * count
    rows_up = 4 * (-(-capacity // 16) * 16)
    hbm = pl.BlockSpec(memory_space=pl.ANY)
    return pl.pallas_call(
        functools.partial(exchange_body, count, capacity),
        out_shape=jax.ShapeDtypeStruct((tokens, width), BF16),
        in_specs=[hbm] * 8,
        out_specs=hbm,
        scratch_shapes=[
            pltpu.VMEM((tokens, width), BF16),
            pltpu.VMEM((2 * tokens, width), BF16),
            pltpu.VMEM((1, width), F32),
            pltpu.VMEM((count, width), BF16),
            pltpu.VMEM(ids.shape, jnp.int32),
            pltpu.VMEM((tokens, LANES), F32),
            pltpu.VMEM((8, tokens), jnp.int32),
            pltpu.VMEM((16, tokens), F32),
            pltpu.VMEM((tokens, LANES), F32),
            pltpu.VMEM((tokens, width), F32),
            pltpu.VMEM((tokens, width), BF16),
            pltpu.VMEM((count, tall, width), BF16),
            pltpu.VMEM((2, count, tall, quarter), BF16),
            pltpu.VMEM((width, 2 * units), BF16),
            pltpu.VMEM((units, width), BF16),
            pltpu.VMEM((count, 4, tall, width), BF16),
            pltpu.VMEM((count, rows_up, 3 * units), F32),
            pltpu.VMEM((count, 4 * capacity, 2 * units), BF16),
            pltpu.VMEM((pieces, 2, 2, tall, quarter), BF16),
            pltpu.VMEM((pieces, 2, tall, quarter), BF16),
            pltpu.VMEM((pieces, tall, quarter), BF16),
            pltpu.VMEM((pieces, tall, quarter), BF16),
            pltpu.VMEM((pieces, tall, quarter), BF16),
            pltpu.VMEM((count, LANES), F32),
            pltpu.VMEM((3, count, LANES), F32),
            pltpu.VMEM((count, LANES), F32),
            pltpu.VMEM((count, count, LANES), F32),
            pltpu.VMEM((count, LANES), F32),
            pltpu.VMEM((tokens, LANES), F32),
            pltpu.SemaphoreType.DMA((3,)),
            pltpu.SemaphoreType.DMA((5,)),
            pltpu.SemaphoreType.DMA((tokens // 32,)),
            pltpu.SemaphoreType.DMA((7, pieces)),
            pltpu.SemaphoreType.DMA((7, pieces)),
            pltpu.SemaphoreType.DMA((2 + count,)),
            pltpu.SemaphoreType.DMA((2 + count,)),
        ],
        compiler_params=pltpu.CompilerParams(
            collective_id=0, has_side_effects=True, vmem_limit_bytes=58 * 2**20
        ),
    )(hidden_states, upstream, gain, router, ids, w_gate, w_up, w_down)


def per_device(hidden_states, upstream, norm_gain, router, expert_ids, w_gate, w_up, w_down):
    tok_rows, model_width = hidden_states.shape
    experts = router.shape[1]
    capacity = 3 * tok_rows // (2 * experts)
    slot_total = experts * capacity
    if (
        capacity == 24 and experts == 8 and lax.axis_size("exp") == 4 and tok_rows == LANES
        and model_width % 1024 == 0
    ):
        return exchange_kernel(
            capacity, hidden_states, upstream, norm_gain[None, :], router.T, expert_ids.T,
            w_gate, w_up, w_down,
        )
    labels = jnp.arange(experts, dtype=jnp.int32)
    chosen = (expert_ids[:, :, None] == labels).astype(F32)
    primary = chosen[:, 0, :]
    member = jnp.sum(chosen, axis=1)
    lower = (
        jnp.arange(tok_rows)[:, None] > jnp.arange(tok_rows)[None, :]
    ).astype(BF16)
    before = jnp.dot(lower, primary.astype(BF16), preferred_element_type=F32)
    slot_index = jnp.sum(before * primary, axis=1).astype(jnp.int32)
    target = expert_ids[:, 0] * capacity + slot_index

    widened = hidden_states.astype(F32)
    inverse = lax.rsqrt(jnp.mean(widened * widened, axis=1, keepdims=True) + EPSILON)
    normed = (widened * inverse * norm_gain).astype(BF16)

    slots_up = pick(target, slot_total, upstream).reshape(experts, capacity, model_width)
    slots_normed = pick(target, slot_total, normed).reshape(experts, capacity, model_width)
    returned, dots = exchange_collective(
        slots_normed, slots_up, w_gate[0], w_up[0], w_down[0]
    )
    own = target[:, None] == jnp.arange(slot_total, dtype=jnp.int32)[None, :]
    raw_back = jnp.dot(own.astype(BF16), returned, preferred_element_type=F32)
    gate_grad = jnp.sum(jnp.where(own, dots[None, :], 0.0), axis=1)

    logits = jnp.dot(normed, router, preferred_element_type=F32)
    probability = jax.nn.softmax(logits, axis=1)
    top_prob = jnp.sum(probability * primary, axis=1)
    route_mass = jnp.sum(probability * member, axis=1)
    gate_value = top_prob / route_mass

    expert_grad = gate_value[:, None] * raw_back
    prob_grad = gate_grad[:, None] * (
        primary / route_mass[:, None] - (top_prob / (route_mass * route_mass))[:, None] * member
    )
    logit_grad = probability * (prob_grad - jnp.sum(probability * prob_grad, axis=1, keepdims=True))
    normed_grad = expert_grad + jnp.dot(
        logit_grad, router.astype(F32).T, precision=lax.Precision.HIGHEST
    )
    scaled = normed_grad * norm_gain
    grad_input = (
        inverse * scaled
        - widened * inverse**3 * jnp.sum(scaled * widened, axis=1, keepdims=True) / model_width
    )
    return grad_input.astype(BF16)


def solution(mesh):
    placed = (
        P(("ctx", "exp"), None),
        P(("ctx", "exp"), None),
        P(),
        P(),
        P(("ctx", "exp"), None),
        P("ctx", None, "exp"),
        P("ctx", None, "exp"),
        P("ctx", "exp", None),
    )
    return jax.shard_map(
        per_device, mesh=mesh, in_specs=placed, out_specs=P(("ctx", "exp"), None), check_vma=False
    )
```

```python
import functools

import jax
import jax.numpy as jnp
from jax import lax
from jax.experimental import pallas as pl
from jax.experimental.pallas import tpu as pltpu
from jax.sharding import PartitionSpec as P

EPSILON = 1e-06
F32 = jnp.float32
BF16 = jnp.bfloat16
LANES = 128


def pick(rows_of, total, values):
    hot = (rows_of[None, :] == jnp.arange(total, dtype=jnp.int32)[:, None]).astype(BF16)
    return jnp.dot(hot, values, preferred_element_type=F32).astype(BF16)


def expert_math(normed_rows, up_rows, gate_block, up_block, down_block):
    pre_gate = jnp.dot(normed_rows, gate_block, preferred_element_type=F32)
    pre_up = jnp.dot(normed_rows, up_block, preferred_element_type=F32)
    raw_grad = lax.dot_general(
        up_rows, down_block, (((1,), (1,)), ((), ())), preferred_element_type=F32
    )
    sig = jax.nn.sigmoid(pre_gate)
    act = pre_gate * sig
    slope = sig * (1.0 + pre_gate * (1.0 - sig))
    hidden = (act * pre_up).astype(BF16).astype(F32)
    dots = jnp.sum(hidden * raw_grad, axis=1)
    grad_gate = (raw_grad * pre_up * slope).astype(BF16)
    grad_up = (raw_grad * act).astype(BF16)
    back = lax.dot_general(
        grad_gate, gate_block, (((1,), (1,)), ((), ())), preferred_element_type=F32
    ) + lax.dot_general(grad_up, up_block, (((1,), (1,)), ((), ())), preferred_element_type=F32)
    return back, dots


def exchange_collective(slots_normed, slots_up, gate_block, up_block, down_block):
    experts, capacity, width = slots_normed.shape

    def dispatch(shaped):
        moved = lax.all_to_all(shaped, "ctx", split_axis=0, concat_axis=0, tiled=True)
        return lax.all_gather(
            moved.reshape(experts * capacity, width), "exp", axis=0, tiled=True
        )

    back, dots = expert_math(
        dispatch(slots_normed), dispatch(slots_up), gate_block, up_block, down_block
    )
    summed = lax.psum_scatter(back.astype(BF16), "exp", scatter_dimension=0, tiled=True)
    dot_sum = lax.psum_scatter(dots, "exp", scatter_dimension=0, tiled=True)
    returned = lax.all_to_all(
        summed.reshape(experts, capacity, width), "ctx", split_axis=0, concat_axis=0, tiled=True
    )
    dot_back = lax.all_to_all(
        dot_sum.reshape(experts, capacity), "ctx", split_axis=0, concat_axis=0, tiled=True
    )
    return returned.reshape(experts * capacity, width), dot_back.reshape(experts * capacity)


def exclusive_or(left, right, count):
    total, bit = 0, 1
    while bit < count:
        total = total + bit * lax.rem(lax.div(left, bit) + lax.div(right, bit), 2)
        bit *= 2
    return total


SEND, ACROSS, RELAY, FORWARD, SLOPES, BACK, SUM, FINISH, WEIGHTS, DOTS, TOTALS, PICK, PROBS = range(13)
SCHEDULE = (
    176, 16, 8, 17, 178, 2, 180, 4, 9, 192, 128, 3, 5, 18, 32, 19, 48, 24,
    34, 182, 10, 50, 35, 25, 21, 33, 51, 11, 7, 66, 82, 20, 49, 40, 64, 80,
    41, 26, 81, 12, 56, 57, 37, 72, 6, 98, 88, 36, 27, 53, 13, 52, 23, 42,
    89, 68, 58, 28, 43, 84, 22, 83, 39, 14, 59, 74, 90, 114, 29, 91, 55, 15,
    38, 44, 104, 105, 85, 54, 107, 45, 60, 30, 70, 61, 120, 86, 106, 76, 121, 87,
    31, 92, 93, 122, 123, 108, 46, 103, 47, 102, 62, 109, 63, 78, 144, 124, 99, 94,
    119, 101, 160, 110, 125, 118, 95, 115, 100, 111, 126, 117, 127, 96, 97, 116, 112, 113,
)


def scheduled(step):
    at, inner = lax.div(step, 3), lax.rem(step, 3)
    word = jnp.int32(0)
    for place in range(0, len(SCHEDULE), 3):
        packed = sum(code * 256**i for i, code in enumerate(SCHEDULE[place : place + 3]))
        word = jnp.where(at == place // 3, jnp.int32(packed), word)
    word = jnp.where(
        inner == 0, word, jnp.where(inner == 1, lax.div(word, 256), lax.div(word, 65536))
    )
    return lax.rem(word, 256)


def exchange_body(
    count, capacity, hidden_hbm, upstream_hbm, gain_hbm, router_hbm, ids_hbm,
    gate_hbm, up_hbm, down_hbm, out_ref,
    hidden, pair, gain, router, ids, inverse, routed, stats, turned, send, landing,
    both, down, rows, acc, grads, part, mate_in, mid, cross_in, done,
    dots, dots_in, dots_sum, dots_back, dots_all, total,
    weight_sem, local_sem, send_sem, recv_sem, tiny_send, tiny_recv,
):
    tokens, width = hidden.shape
    half = width // 2
    quarter = width // 4
    units = down.shape[0]
    tall = -(-capacity // 16) * 16
    skip = tall - capacity
    ctx = lax.axis_index("ctx")
    exp = lax.axis_index("exp")
    row, core = lax.div(exp, 2), lax.rem(exp, 2)
    mate = row * 2 + (1 - core)
    cross = (1 - row) * 2 + core
    diagonal = (1 - row) * 2 + (1 - core)
    peers = (mate, cross, diagonal)

    def remote(src, dst, send, recv, device):
        return pltpu.make_async_remote_copy(
            src_ref=src, dst_ref=dst, send_sem=send, recv_sem=recv,
            device_id=device, device_id_type=pl.DeviceIdType.MESH,
        )

    def piece(kind, src, dst, c, device):
        return remote(src, dst, send_sem.at[kind, c], recv_sem.at[kind, c], device)

    def partner(k):
        return exclusive_or(ctx, k, count)

    def side(h):
        return pl.ds(pl.multiple_of(h * half, half), half)

    def direct(k, h):
        return piece(
            0, send.at[k, :, side(h)], rows.at[k, exp, :, side(h)], 2 * k + h,
            (partner(k), exp),
        )

    def to_mate(k, h):
        own = rows.at[k, exp, :, side(h)]
        return piece(1, own, own, 2 * k + h, (ctx, mate))

    def to_cross(k, h):
        own = rows.at[k, exp, :, side(h)]
        return piece(2, own, own, 2 * k + h, (ctx, cross))

    def relay(k, h):
        own = rows.at[k, cross, :, side(h)]
        return piece(3, own, own, 2 * k + h, (ctx, mate))

    def part_to_mate(c):
        return piece(4, part.at[c, 1 - core], mate_in.at[c], c, (ctx, mate))

    def sum_to_cross(c):
        return piece(5, mid.at[c], cross_in.at[c], c, (ctx, cross))

    def give_back(k, h):
        return piece(
            6, done.at[2 * k + h], landing.at[h, ctx], 2 * k + h, (partner(k), exp)
        )

    def dots_to(q):
        return remote(dots, dots_in.at[q], tiny_send.at[q], tiny_recv.at[q], (ctx, peers[q]))

    def totals_to(k):
        return remote(
            dots_sum, dots_back.at[k], tiny_send.at[2 + k], tiny_recv.at[2 + k],
            (partner(k), exp),
        )

    weights = [
        pltpu.make_async_copy(gate_hbm.at[0], both.at[:, pl.ds(0, units)], weight_sem.at[0]),
        pltpu.make_async_copy(up_hbm.at[0], both.at[:, pl.ds(units, units)], weight_sem.at[1]),
        pltpu.make_async_copy(down_hbm.at[0], down, weight_sem.at[2]),
    ]
    loads = [
        pltpu.make_async_copy(ids_hbm, ids, local_sem.at[0]),
        pltpu.make_async_copy(gain_hbm, gain, local_sem.at[1]),
        pltpu.make_async_copy(hidden_hbm, hidden, local_sem.at[2]),
        pltpu.make_async_copy(upstream_hbm, pair.at[pl.ds(tokens, tokens)], local_sem.at[3]),
        pltpu.make_async_copy(router_hbm, router, local_sem.at[4]),
    ]
    for copy in loads:
        copy.start()
    barrier = pltpu.get_barrier_semaphore()

    @pl.loop(1, count)
    def _(k):
        pl.semaphore_signal(
            barrier, inc=1, device_id=(partner(k), exp), device_id_type=pl.DeviceIdType.MESH
        )

    for other in peers:
        pl.semaphore_signal(
            barrier, inc=1, device_id=(ctx, other), device_id_type=pl.DeviceIdType.MESH
        )
    dots[...] = jnp.zeros_like(dots)
    loads[0].wait()
    experts = lax.broadcasted_iota(jnp.int32, (count, tokens), 0)
    first = ids[pl.ds(0, 1), :]
    primary = (first == experts).astype(F32)
    earlier = (
        lax.broadcasted_iota(jnp.int32, (tokens, tokens), 0)
        < lax.broadcasted_iota(jnp.int32, (tokens, tokens), 1)
    ).astype(BF16)
    before = jnp.dot(primary.astype(BF16), earlier, preferred_element_type=F32)
    slot = jnp.sum(before * primary, axis=0, keepdims=True).astype(jnp.int32)
    routed[pl.ds(0, 1), :] = slot

    loads[1].wait()
    loads[2].wait()

    @pl.loop(0, tokens // 16)
    def _(i):
        some = pl.ds(pl.multiple_of(i * 16, 16), 16)
        wide = hidden[some, :].astype(F32)
        scale = lax.rsqrt(jnp.mean(wide * wide, axis=1, keepdims=True) + EPSILON)
        inverse[some, :] = jnp.broadcast_to(scale, (16, LANES))
        pair[some, :] = (wide * scale * gain[...]).astype(BF16)

    loads[3].wait()
    for copy in weights:
        copy.start()

    def pick_rows(k):
        inner = lax.broadcasted_iota(jnp.int32, (2 * capacity, 2 * tokens), 0)
        token = lax.broadcasted_iota(jnp.int32, (2 * capacity, 2 * tokens), 1)
        place = jnp.where(
            ids[pl.ds(0, 1), :] == partner(k), routed[pl.ds(0, 1), :], -2 * capacity
        )
        wanted = jnp.concatenate([place, place + capacity], axis=1)
        upper = (token >= tokens) == (inner >= capacity)
        return jnp.logical_and(wanted == inner, upper).astype(F32)

    def pick(k):
        hot = jnp.concatenate([pick_rows(k), pick_rows(k + 4)], axis=0).astype(BF16)

        @pl.loop(0, 4)
        def _(j):
            columns = pl.ds(pl.multiple_of(j * quarter, quarter), quarter)
            found = jnp.dot(hot, pair[:, columns], preferred_element_type=F32).astype(BF16)

            @pl.when(k == 0)
            def _():
                rows[0, exp, :, columns] = found[: 2 * capacity]

            @pl.when(k > 0)
            def _():
                send[k, :, columns] = found[: 2 * capacity]

            send[k + 4, :, columns] = found[2 * capacity :]

    def shares():
        ids_all = ids[...]
        labels = lax.broadcasted_iota(jnp.int32, (count, tokens), 0)
        logits = lax.dot_general(
            router[...], pair[pl.ds(0, tokens), :], (((1,), (1,)), ((), ())),
            preferred_element_type=F32,
        )
        raised = jnp.exp(logits - jnp.max(logits, axis=0, keepdims=True))
        probability = raised / jnp.sum(raised, axis=0, keepdims=True)
        primary = (ids_all[:1] == labels).astype(F32)
        member = jnp.zeros((count, tokens), F32)
        for one in range(ids.shape[0]):
            member = member + (ids_all[one : one + 1] == labels).astype(F32)
        top_prob = jnp.sum(probability * primary, axis=0, keepdims=True)
        route_mass = jnp.sum(probability * member, axis=0, keepdims=True)
        return probability, primary, member, top_prob, route_mass

    pl.semaphore_wait(barrier, count + 2)

    @pl.loop(0, len(SCHEDULE))
    def _(step):
        code = scheduled(step)
        kind = lax.div(code, 16)
        c = lax.rem(code, 16)
        k = lax.div(c, 2)
        h = lax.rem(c, 2)

        @pl.when(kind == SEND)
        def _():
            direct(k, h).start()

        @pl.when(jnp.logical_and(kind == ACROSS, k > 0))
        def _():
            direct(k, h).wait_recv()

        @pl.when(kind == ACROSS)
        def _():
            to_cross(k, h).start()
            to_mate(k, h).start()

        @pl.when(kind == RELAY)
        def _():
            to_cross(k, h).wait_recv()
            relay(k, h).start()

        @pl.when(kind == PICK)
        def _():
            pick(k)

        @pl.when(kind == PROBS)
        def _():
            loads[4].wait()
            probability, primary, member, top_prob, route_mass = shares()
            place = ids[pl.ds(0, 1), :] * (2 * capacity) + routed[pl.ds(0, 1), :]
            stats[pl.ds(0, 8), :] = probability
            stats[pl.ds(8, 8), :] = primary / route_mass - (
                top_prob / (route_mass * route_mass)
            ) * member
            lines = jnp.concatenate(
                [
                    jnp.broadcast_to(top_prob / route_mass, (8, tokens)),
                    jnp.broadcast_to(place.astype(F32), (8, tokens)),
                    jnp.zeros((LANES - 16, tokens), F32),
                ],
                axis=0,
            )
            turned[...] = lines.T

        @pl.when(kind == WEIGHTS)
        def _():
            for copy in weights:
                copy.wait()
            acc[...] = jnp.zeros_like(acc)

        @pl.when(kind == FORWARD)
        def _():
            to_mate(k, h).wait_recv()
            relay(k, h).wait_recv()
            columns = side(h)
            acc[k, :, pl.ds(0, 2 * units)] += jnp.dot(
                rows[k, :, pl.ds(0, tall), columns].reshape(4 * tall, half),
                both[columns, :],
                preferred_element_type=F32,
            )
            acc[k, :, pl.ds(2 * units, units)] += lax.dot_general(
                rows[k, :, pl.ds(2 * capacity - tall, tall), columns].reshape(4 * tall, half),
                down[:, columns],
                (((1,), (1,)), ((), ())),
                preferred_element_type=F32,
            )

        @pl.when(kind == SLOPES)
        def _():
            pre_gate = acc[k, :, pl.ds(0, units)].reshape(4, tall, units)[:, :capacity]
            pre_up = acc[k, :, pl.ds(units, units)].reshape(4, tall, units)[:, :capacity]
            raw_grad = acc[k, :, pl.ds(2 * units, units)].reshape(4, tall, units)[:, skip:]
            sig = jax.nn.sigmoid(pre_gate)
            act = pre_gate * sig
            slope = sig * (1.0 + pre_gate * (1.0 - sig))
            hidden = (act * pre_up).astype(BF16).astype(F32)
            terms = (hidden * raw_grad).reshape(4 * capacity, units)
            high = terms.astype(BF16)
            low = (terms - high.astype(F32)).astype(BF16)
            ones = jnp.ones((8, units), BF16)
            lined = lax.dot_general(
                ones, high, (((1,), (1,)), ((), ())), preferred_element_type=F32
            ) + lax.dot_general(ones, low, (((1,), (1,)), ((), ())), preferred_element_type=F32)
            dots[pl.ds(k, 1), pl.ds(0, 4 * capacity)] = lined[:1]
            grads[k, :, pl.ds(0, units)] = (
                (raw_grad * pre_up * slope).reshape(4 * capacity, units).astype(BF16)
            )
            grads[k, :, pl.ds(units, units)] = (
                (raw_grad * act).reshape(4 * capacity, units).astype(BF16)
            )

        @pl.when(kind == BACK)
        def _():
            sides = []
            for side_index in range(2):
                start = pl.multiple_of(side_index * half + h * quarter, quarter)
                product = lax.dot_general(
                    grads[k],
                    both[pl.ds(start, quarter), :],
                    (((1,), (1,)), ((), ())),
                    preferred_element_type=F32,
                )
                sides.append(product.reshape(4, capacity, quarter))
            value = jnp.concatenate(sides, axis=1).astype(BF16)
            for one in range(4):
                part[c, one % 2, one // 2] = value[one]
            part_to_mate(c).start()

        @pl.when(kind == SUM)
        def _():
            part_to_mate(c).wait_recv()
            total = part[c, core, 1 - row].astype(F32) + mate_in[c, 1 - row].astype(F32)
            mid[c] = total.astype(BF16)
            sum_to_cross(c).start()

        @pl.when(kind == FINISH)
        def _():
            sum_to_cross(c).wait_recv()
            total = part[c, core, row].astype(F32) + mate_in[c, row].astype(F32)
            total = (total + cross_in[c].astype(F32)).astype(BF16)

            @pl.when(k == 0)
            def _():
                landing[h, ctx] = total

            @pl.when(k > 0)
            def _():
                done[c] = total
                give_back(k, h).start()

        @pl.when(kind == DOTS)
        def _():
            for q in range(3):
                dots_to(q).start()

        @pl.when(kind == TOTALS)
        def _():
            for q in range(3):
                dots_to(q).wait_recv()
            dots_sum[...] = dots[...] + dots_in[0] + dots_in[1] + dots_in[2]

            @pl.loop(1, count)
            def _(k):
                totals_to(k).start()

    dots_all[pl.ds(ctx, 1), :] = dots_sum[:1]

    @pl.loop(1, count)
    def _(k):
        totals_to(k).wait()
        dots_all[pl.ds(partner(k), 1), :] = dots_back[k, pl.ds(k, 1), :]

    at = lax.broadcasted_iota(jnp.int32, (LANES, tokens), 0)
    here = (at == routed[pl.ds(0, 1), :] + exp * capacity).astype(BF16)
    gathered = jnp.zeros((count, tokens), F32)
    rest = dots_all[...]
    for _ in range(3):
        high = rest.astype(BF16)
        rest = rest - high.astype(F32)
        gathered = gathered + jnp.dot(high, here, preferred_element_type=F32)
    labels = lax.broadcasted_iota(jnp.int32, (count, tokens), 0)
    gate_grad = jnp.sum(
        jnp.where(ids[pl.ds(0, 1), :] == labels, gathered, 0.0), axis=0, keepdims=True
    )
    probability = stats[pl.ds(0, 8), :]
    prob_grad = gate_grad * stats[pl.ds(8, 8), :]
    logit_grad = probability * (
        prob_grad - jnp.sum(probability * prob_grad, axis=0, keepdims=True)
    )
    high = logit_grad.astype(BF16).astype(F32)
    middle = (logit_grad - high).astype(BF16).astype(F32)
    low = logit_grad - high - middle
    lines = jnp.concatenate(
        [high, middle, low, jnp.zeros((LANES - 24, tokens), F32)], axis=0
    )
    logit_lines = lines.T.astype(BF16)
    gate = turned[:, pl.ds(0, 1)]
    place = turned[:, pl.ds(8, 1)].astype(jnp.int32)
    spot = lax.broadcasted_iota(jnp.int32, (tokens, 2 * capacity * count), 1)
    thrice = jnp.concatenate(
        [router[...].astype(F32)] * 3 + [jnp.zeros((LANES - 24, width), F32)], axis=0
    ).astype(BF16)
    total[...] = jnp.zeros_like(total)
    for h in range(2):

        @pl.loop(1, count)
        def _(k):
            give_back(k, h).wait_recv()

        found = landing[h].reshape(2 * capacity * count, quarter)
        for half_index in range(2):
            start = half_index * half + h * quarter
            columns = pl.ds(start, quarter)
            own = (place + half_index * capacity == spot).astype(BF16)
            back = gate * jnp.dot(own, found, preferred_element_type=F32)
            back = back + jnp.dot(
                logit_lines, thrice[:, start : start + quarter], preferred_element_type=F32
            )
            back = back * gain[:, columns]
            acc[2 * half_index + h, :, pl.ds(0, quarter)] = back
            along = back * hidden[:, columns].astype(F32)
            some = along[:, :LANES]
            for one in range(1, quarter // LANES):
                some = some + along[:, one * LANES : (one + 1) * LANES]
            total[...] += some

    @pl.loop(0, tokens // 32)
    def _(i):
        some = pl.ds(pl.multiple_of(i * 32, 32), 32)
        factor = inverse[some, pl.ds(0, 1)]
        weight = jnp.sum(total[some, :], axis=1, keepdims=True) * factor**3 / width
        for block in range(4):
            columns = pl.ds(block * quarter, quarter)
            out_ref[some, columns] = (
                factor * acc[block, some, pl.ds(0, quarter)]
                - hidden[some, columns].astype(F32) * weight
            ).astype(BF16)

    for q in range(3):
        dots_to(q).wait_send()

    @pl.loop(0, 2 * count)
    def _(c):
        k, h = lax.div(c, 2), lax.rem(c, 2)
        to_mate(k, h).wait_send()
        to_cross(k, h).wait_send()
        relay(k, h).wait_send()
        part_to_mate(c).wait_send()
        sum_to_cross(c).wait_send()

        @pl.when(k > 0)
        def _():
            direct(k, h).wait_send()
            give_back(k, h).wait_send()


def exchange_kernel(capacity, hidden_states, upstream, gain, router, ids, w_gate, w_up, w_down):
    tokens, width = hidden_states.shape
    count, tall = router.shape[0], 2 * capacity
    units = w_down.shape[1]
    quarter = width // 4
    pieces = 2 * count
    rows_up = 4 * (-(-capacity // 16) * 16)
    hbm = pl.BlockSpec(memory_space=pl.ANY)
    return pl.pallas_call(
        functools.partial(exchange_body, count, capacity),
        out_shape=jax.ShapeDtypeStruct((tokens, width), BF16),
        in_specs=[hbm] * 8,
        out_specs=pl.BlockSpec(memory_space=pltpu.VMEM),
        scratch_shapes=[
            pltpu.VMEM((tokens, width), BF16),
            pltpu.VMEM((2 * tokens, width), BF16),
            pltpu.VMEM((1, width), F32),
            pltpu.VMEM((count, width), BF16),
            pltpu.VMEM(ids.shape, jnp.int32),
            pltpu.VMEM((tokens, LANES), F32),
            pltpu.VMEM((8, tokens), jnp.int32),
            pltpu.VMEM((16, tokens), F32),
            pltpu.VMEM((tokens, LANES), F32),
            pltpu.VMEM((count, tall, width), BF16),
            pltpu.VMEM((2, count, tall, quarter), BF16),
            pltpu.VMEM((width, 2 * units), BF16),
            pltpu.VMEM((units, width), BF16),
            pltpu.VMEM((count, 4, tall, width), BF16),
            pltpu.VMEM((count, rows_up, 3 * units), F32),
            pltpu.VMEM((count, 4 * capacity, 2 * units), BF16),
            pltpu.VMEM((pieces, 2, 2, tall, quarter), BF16),
            pltpu.VMEM((pieces, 2, tall, quarter), BF16),
            pltpu.VMEM((pieces, tall, quarter), BF16),
            pltpu.VMEM((pieces, tall, quarter), BF16),
            pltpu.VMEM((pieces, tall, quarter), BF16),
            pltpu.VMEM((count, LANES), F32),
            pltpu.VMEM((3, count, LANES), F32),
            pltpu.VMEM((count, LANES), F32),
            pltpu.VMEM((count, count, LANES), F32),
            pltpu.VMEM((count, LANES), F32),
            pltpu.VMEM((tokens, LANES), F32),
            pltpu.SemaphoreType.DMA((3,)),
            pltpu.SemaphoreType.DMA((5,)),
            pltpu.SemaphoreType.DMA((7, pieces)),
            pltpu.SemaphoreType.DMA((7, pieces)),
            pltpu.SemaphoreType.DMA((2 + count,)),
            pltpu.SemaphoreType.DMA((2 + count,)),
        ],
        compiler_params=pltpu.CompilerParams(
            collective_id=0, has_side_effects=True, vmem_limit_bytes=52 * 2**20
        ),
    )(
        *(
            pltpu.with_memory_space_constraint(one, pltpu.HBM)
            for one in (hidden_states, upstream, gain, router, ids, w_gate, w_up, w_down)
        )
    )


def per_device(hidden_states, upstream, norm_gain, router, expert_ids, w_gate, w_up, w_down):
    tok_rows, model_width = hidden_states.shape
    experts = router.shape[1]
    capacity = 3 * tok_rows // (2 * experts)
    slot_total = experts * capacity
    if (
        capacity == 24 and experts == 8 and lax.axis_size("exp") == 4 and tok_rows == LANES
        and model_width % 1024 == 0
    ):
        return exchange_kernel(
            capacity, hidden_states, upstream, norm_gain[None, :], router.T, expert_ids.T,
            w_gate, w_up, w_down,
        )
    labels = jnp.arange(experts, dtype=jnp.int32)
    chosen = (expert_ids[:, :, None] == labels).astype(F32)
    primary = chosen[:, 0, :]
    member = jnp.sum(chosen, axis=1)
    lower = (
        jnp.arange(tok_rows)[:, None] > jnp.arange(tok_rows)[None, :]
    ).astype(BF16)
    before = jnp.dot(lower, primary.astype(BF16), preferred_element_type=F32)
    slot_index = jnp.sum(before * primary, axis=1).astype(jnp.int32)
    target = expert_ids[:, 0] * capacity + slot_index

    widened = hidden_states.astype(F32)
    inverse = lax.rsqrt(jnp.mean(widened * widened, axis=1, keepdims=True) + EPSILON)
    normed = (widened * inverse * norm_gain).astype(BF16)

    slots_up = pick(target, slot_total, upstream).reshape(experts, capacity, model_width)
    slots_normed = pick(target, slot_total, normed).reshape(experts, capacity, model_width)
    returned, dots = exchange_collective(
        slots_normed, slots_up, w_gate[0], w_up[0], w_down[0]
    )
    own = target[:, None] == jnp.arange(slot_total, dtype=jnp.int32)[None, :]
    raw_back = jnp.dot(own.astype(BF16), returned, preferred_element_type=F32)
    gate_grad = jnp.sum(jnp.where(own, dots[None, :], 0.0), axis=1)

    logits = jnp.dot(normed, router, preferred_element_type=F32)
    probability = jax.nn.softmax(logits, axis=1)
    top_prob = jnp.sum(probability * primary, axis=1)
    route_mass = jnp.sum(probability * member, axis=1)
    gate_value = top_prob / route_mass

    expert_grad = gate_value[:, None] * raw_back
    prob_grad = gate_grad[:, None] * (
        primary / route_mass[:, None] - (top_prob / (route_mass * route_mass))[:, None] * member
    )
    logit_grad = probability * (prob_grad - jnp.sum(probability * prob_grad, axis=1, keepdims=True))
    normed_grad = expert_grad + jnp.dot(
        logit_grad, router.astype(F32).T, precision=lax.Precision.HIGHEST
    )
    scaled = normed_grad * norm_gain
    grad_input = (
        inverse * scaled
        - widened * inverse**3 * jnp.sum(scaled * widened, axis=1, keepdims=True) / model_width
    )
    return grad_input.astype(BF16)


def solution(mesh):
    placed = (
        P(("ctx", "exp"), None),
        P(("ctx", "exp"), None),
        P(),
        P(),
        P(("ctx", "exp"), None),
        P("ctx", None, "exp"),
        P("ctx", None, "exp"),
        P("ctx", "exp", None),
    )
    return jax.shard_map(
        per_device, mesh=mesh, in_specs=placed, out_specs=P(("ctx", "exp"), None), check_vma=False
    )
```

```python
import functools

import jax
import jax.numpy as jnp
from jax import lax
from jax.experimental import pallas as pl
from jax.experimental.pallas import tpu as pltpu
from jax.sharding import PartitionSpec as P

EPSILON = 1e-06
F32 = jnp.float32
BF16 = jnp.bfloat16
LANES = 128


def pick(rows_of, total, values):
    hot = (rows_of[None, :] == jnp.arange(total, dtype=jnp.int32)[:, None]).astype(BF16)
    return jnp.dot(hot, values, preferred_element_type=F32).astype(BF16)


def expert_math(normed_rows, up_rows, gate_block, up_block, down_block):
    pre_gate = jnp.dot(normed_rows, gate_block, preferred_element_type=F32)
    pre_up = jnp.dot(normed_rows, up_block, preferred_element_type=F32)
    raw_grad = lax.dot_general(
        up_rows, down_block, (((1,), (1,)), ((), ())), preferred_element_type=F32
    )
    sig = jax.nn.sigmoid(pre_gate)
    act = pre_gate * sig
    slope = sig * (1.0 + pre_gate * (1.0 - sig))
    hidden = (act * pre_up).astype(BF16).astype(F32)
    dots = jnp.sum(hidden * raw_grad, axis=1)
    grad_gate = (raw_grad * pre_up * slope).astype(BF16)
    grad_up = (raw_grad * act).astype(BF16)
    back = lax.dot_general(
        grad_gate, gate_block, (((1,), (1,)), ((), ())), preferred_element_type=F32
    ) + lax.dot_general(grad_up, up_block, (((1,), (1,)), ((), ())), preferred_element_type=F32)
    return back, dots


def exchange_collective(slots_normed, slots_up, gate_block, up_block, down_block):
    experts, capacity, width = slots_normed.shape

    def dispatch(shaped):
        moved = lax.all_to_all(shaped, "ctx", split_axis=0, concat_axis=0, tiled=True)
        return lax.all_gather(
            moved.reshape(experts * capacity, width), "exp", axis=0, tiled=True
        )

    back, dots = expert_math(
        dispatch(slots_normed), dispatch(slots_up), gate_block, up_block, down_block
    )
    summed = lax.psum_scatter(back.astype(BF16), "exp", scatter_dimension=0, tiled=True)
    dot_sum = lax.psum_scatter(dots, "exp", scatter_dimension=0, tiled=True)
    returned = lax.all_to_all(
        summed.reshape(experts, capacity, width), "ctx", split_axis=0, concat_axis=0, tiled=True
    )
    dot_back = lax.all_to_all(
        dot_sum.reshape(experts, capacity), "ctx", split_axis=0, concat_axis=0, tiled=True
    )
    return returned.reshape(experts * capacity, width), dot_back.reshape(experts * capacity)


def exclusive_or(left, right, count):
    total, bit = 0, 1
    while bit < count:
        total = total + bit * lax.rem(lax.div(left, bit) + lax.div(right, bit), 2)
        bit *= 2
    return total


SEND, ACROSS, RELAY, FORWARD, SLOPES, BACK, SUM, FINISH, WEIGHTS, DOTS, TOTALS, PICK, PROBS = range(13)
SCHEDULE = (
    176, 16, 8, 177, 17, 178, 2, 180, 4, 9, 192, 128, 179, 3, 181, 5, 18, 32,
    19, 48, 24, 34, 10, 50, 35, 25, 21, 33, 51, 11, 66, 82, 20, 183, 7, 49,
    40, 64, 80, 41, 26, 81, 12, 56, 57, 37, 72, 98, 88, 36, 27, 53, 13, 52,
    23, 182, 6, 42, 89, 68, 58, 28, 43, 84, 22, 83, 14, 39, 59, 74, 90, 29,
    91, 55, 114, 15, 38, 44, 104, 105, 85, 54, 107, 45, 60, 30, 70, 61, 120, 86,
    106, 76, 121, 87, 31, 92, 93, 122, 123, 108, 46, 103, 47, 102, 62, 109, 63, 124,
    78, 144, 99, 94, 110, 119, 101, 160, 125, 118, 95, 111, 115, 100, 126, 117, 127, 96,
    97, 116, 112, 113,
)


def scheduled(step):
    at, inner = lax.div(step, 3), lax.rem(step, 3)
    word = jnp.int32(0)
    for place in range(0, len(SCHEDULE), 3):
        packed = sum(code * 256**i for i, code in enumerate(SCHEDULE[place : place + 3]))
        word = jnp.where(at == place // 3, jnp.int32(packed), word)
    word = jnp.where(
        inner == 0, word, jnp.where(inner == 1, lax.div(word, 256), lax.div(word, 65536))
    )
    return lax.rem(word, 256)


def exchange_body(
    count, capacity, hidden_hbm, upstream_hbm, gain_hbm, router_hbm, ids_hbm,
    gate_hbm, up_hbm, down_hbm, out_ref,
    hidden, pair, gain, router, ids, inverse, routed, stats, turned, send, landing,
    both, down, rows, acc, grads, part, mate_in, mid, cross_in, done,
    dots, dots_in, dots_sum, dots_back, dots_all, total,
    weight_sem, local_sem, send_sem, recv_sem, tiny_send, tiny_recv,
):
    tokens, width = hidden.shape
    half = width // 2
    quarter = width // 4
    units = down.shape[0]
    tall = -(-capacity // 16) * 16
    skip = tall - capacity
    ctx = lax.axis_index("ctx")
    exp = lax.axis_index("exp")
    row, core = lax.div(exp, 2), lax.rem(exp, 2)
    mate = row * 2 + (1 - core)
    cross = (1 - row) * 2 + core
    diagonal = (1 - row) * 2 + (1 - core)
    peers = (mate, cross, diagonal)

    def remote(src, dst, send, recv, device):
        return pltpu.make_async_remote_copy(
            src_ref=src, dst_ref=dst, send_sem=send, recv_sem=recv,
            device_id=device, device_id_type=pl.DeviceIdType.MESH,
        )

    def piece(kind, src, dst, c, device):
        return remote(src, dst, send_sem.at[kind, c], recv_sem.at[kind, c], device)

    def partner(k):
        return exclusive_or(ctx, k, count)

    def side(h):
        return pl.ds(pl.multiple_of(h * half, half), half)

    def direct(k, h):
        return piece(
            0, send.at[k, :, side(h)], rows.at[k, exp, :, side(h)], 2 * k + h,
            (partner(k), exp),
        )

    def to_mate(k, h):
        own = rows.at[k, exp, :, side(h)]
        return piece(1, own, own, 2 * k + h, (ctx, mate))

    def to_cross(k, h):
        own = rows.at[k, exp, :, side(h)]
        return piece(2, own, own, 2 * k + h, (ctx, cross))

    def relay(k, h):
        own = rows.at[k, cross, :, side(h)]
        return piece(3, own, own, 2 * k + h, (ctx, mate))

    def part_to_mate(c):
        return piece(4, part.at[c, 1 - core], mate_in.at[c], c, (ctx, mate))

    def sum_to_cross(c):
        return piece(5, mid.at[c], cross_in.at[c], c, (ctx, cross))

    def give_back(k, h):
        return piece(
            6, done.at[2 * k + h], landing.at[h, ctx], 2 * k + h, (partner(k), exp)
        )

    def dots_to(q):
        return remote(dots, dots_in.at[q], tiny_send.at[q], tiny_recv.at[q], (ctx, peers[q]))

    def totals_to(k):
        return remote(
            dots_sum, dots_back.at[k], tiny_send.at[2 + k], tiny_recv.at[2 + k],
            (partner(k), exp),
        )

    weights = [
        pltpu.make_async_copy(gate_hbm.at[0], both.at[:, pl.ds(0, units)], weight_sem.at[0]),
        pltpu.make_async_copy(up_hbm.at[0], both.at[:, pl.ds(units, units)], weight_sem.at[1]),
        pltpu.make_async_copy(down_hbm.at[0], down, weight_sem.at[2]),
    ]
    loads = [
        pltpu.make_async_copy(ids_hbm, ids, local_sem.at[0]),
        pltpu.make_async_copy(gain_hbm, gain, local_sem.at[1]),
        pltpu.make_async_copy(router_hbm, router, local_sem.at[2]),
        pltpu.make_async_copy(upstream_hbm, pair.at[pl.ds(tokens, tokens)], local_sem.at[3]),
    ]

    def hidden_copy(i):
        some = pl.ds(pl.multiple_of(i * 32, 32), 32)
        return pltpu.make_async_copy(hidden_hbm.at[some], hidden.at[some], local_sem.at[4 + i])

    for copy in loads[:2]:
        copy.start()
    for i in range(tokens // 32):
        hidden_copy(i).start()
    for copy in loads[2:]:
        copy.start()
    barrier = pltpu.get_barrier_semaphore()

    @pl.loop(1, count)
    def _(k):
        pl.semaphore_signal(
            barrier, inc=1, device_id=(partner(k), exp), device_id_type=pl.DeviceIdType.MESH
        )

    for other in peers:
        pl.semaphore_signal(
            barrier, inc=1, device_id=(ctx, other), device_id_type=pl.DeviceIdType.MESH
        )
    dots[...] = jnp.zeros_like(dots)
    loads[0].wait()
    experts = lax.broadcasted_iota(jnp.int32, (count, tokens), 0)
    first = ids[pl.ds(0, 1), :]
    primary = (first == experts).astype(F32)
    earlier = (
        lax.broadcasted_iota(jnp.int32, (tokens, tokens), 0)
        < lax.broadcasted_iota(jnp.int32, (tokens, tokens), 1)
    ).astype(BF16)
    before = jnp.dot(primary.astype(BF16), earlier, preferred_element_type=F32)
    slot = jnp.sum(before * primary, axis=0, keepdims=True).astype(jnp.int32)
    routed[pl.ds(0, 1), :] = slot

    loads[1].wait()

    @pl.loop(0, tokens // 16)
    def _(i):
        @pl.when(lax.rem(i, 2) == 0)
        def _():
            hidden_copy(lax.div(i, 2)).wait()

        some = pl.ds(pl.multiple_of(i * 16, 16), 16)
        wide = hidden[some, :].astype(F32)
        scale = lax.rsqrt(jnp.mean(wide * wide, axis=1, keepdims=True) + EPSILON)
        inverse[some, :] = jnp.broadcast_to(scale, (16, LANES))
        pair[some, :] = (wide * scale * gain[...]).astype(BF16)

    loads[3].wait()
    for copy in weights:
        copy.start()

    def pick_rows(k):
        inner = lax.broadcasted_iota(jnp.int32, (2 * capacity, 2 * tokens), 0)
        token = lax.broadcasted_iota(jnp.int32, (2 * capacity, 2 * tokens), 1)
        place = jnp.where(
            ids[pl.ds(0, 1), :] == partner(k), routed[pl.ds(0, 1), :], -2 * capacity
        )
        wanted = jnp.concatenate([place, place + capacity], axis=1)
        upper = (token >= tokens) == (inner >= capacity)
        return jnp.logical_and(wanted == inner, upper).astype(F32)

    def pick(k, h):
        hot = jnp.concatenate([pick_rows(k), pick_rows(k + 4)], axis=0).astype(BF16)

        @pl.loop(0, 2)
        def _(j):
            columns = pl.ds(pl.multiple_of(h * half + j * quarter, quarter), quarter)
            found = jnp.dot(hot, pair[:, columns], preferred_element_type=F32).astype(BF16)

            @pl.when(k == 0)
            def _():
                rows[0, exp, :, columns] = found[: 2 * capacity]

            @pl.when(k > 0)
            def _():
                send[k, :, columns] = found[: 2 * capacity]

            send[k + 4, :, columns] = found[2 * capacity :]

    def shares():
        ids_all = ids[...]
        labels = lax.broadcasted_iota(jnp.int32, (count, tokens), 0)
        logits = lax.dot_general(
            router[...], pair[pl.ds(0, tokens), :], (((1,), (1,)), ((), ())),
            preferred_element_type=F32,
        )
        raised = jnp.exp(logits - jnp.max(logits, axis=0, keepdims=True))
        probability = raised / jnp.sum(raised, axis=0, keepdims=True)
        primary = (ids_all[:1] == labels).astype(F32)
        member = jnp.zeros((count, tokens), F32)
        for one in range(ids.shape[0]):
            member = member + (ids_all[one : one + 1] == labels).astype(F32)
        top_prob = jnp.sum(probability * primary, axis=0, keepdims=True)
        route_mass = jnp.sum(probability * member, axis=0, keepdims=True)
        return probability, primary, member, top_prob, route_mass

    pl.semaphore_wait(barrier, count + 2)

    @pl.loop(0, len(SCHEDULE))
    def _(step):
        code = scheduled(step)
        kind = lax.div(code, 16)
        c = lax.rem(code, 16)
        k = lax.div(c, 2)
        h = lax.rem(c, 2)

        @pl.when(kind == SEND)
        def _():
            direct(k, h).start()

        @pl.when(jnp.logical_and(kind == ACROSS, k > 0))
        def _():
            direct(k, h).wait_recv()

        @pl.when(kind == ACROSS)
        def _():
            to_cross(k, h).start()
            to_mate(k, h).start()

        @pl.when(kind == RELAY)
        def _():
            to_cross(k, h).wait_recv()
            relay(k, h).start()

        @pl.when(kind == PICK)
        def _():
            pick(k, h)

        @pl.when(kind == PROBS)
        def _():
            loads[2].wait()
            probability, primary, member, top_prob, route_mass = shares()
            place = ids[pl.ds(0, 1), :] * (2 * capacity) + routed[pl.ds(0, 1), :]
            stats[pl.ds(0, 8), :] = probability
            stats[pl.ds(8, 8), :] = primary / route_mass - (
                top_prob / (route_mass * route_mass)
            ) * member
            lines = jnp.concatenate(
                [
                    jnp.broadcast_to(top_prob / route_mass, (8, tokens)),
                    jnp.broadcast_to(place.astype(F32), (8, tokens)),
                    jnp.zeros((LANES - 16, tokens), F32),
                ],
                axis=0,
            )
            turned[...] = lines.T

        @pl.when(kind == WEIGHTS)
        def _():
            for copy in weights:
                copy.wait()
            acc[...] = jnp.zeros_like(acc)

        @pl.when(kind == FORWARD)
        def _():
            to_mate(k, h).wait_recv()
            relay(k, h).wait_recv()
            columns = side(h)
            acc[k, :, pl.ds(0, 2 * units)] += jnp.dot(
                rows[k, :, pl.ds(0, tall), columns].reshape(4 * tall, half),
                both[columns, :],
                preferred_element_type=F32,
            )
            acc[k, :, pl.ds(2 * units, units)] += lax.dot_general(
                rows[k, :, pl.ds(2 * capacity - tall, tall), columns].reshape(4 * tall, half),
                down[:, columns],
                (((1,), (1,)), ((), ())),
                preferred_element_type=F32,
            )

        @pl.when(kind == SLOPES)
        def _():
            pre_gate = acc[k, :, pl.ds(0, units)].reshape(4, tall, units)[:, :capacity]
            pre_up = acc[k, :, pl.ds(units, units)].reshape(4, tall, units)[:, :capacity]
            raw_grad = acc[k, :, pl.ds(2 * units, units)].reshape(4, tall, units)[:, skip:]
            sig = jax.nn.sigmoid(pre_gate)
            act = pre_gate * sig
            slope = sig * (1.0 + pre_gate * (1.0 - sig))
            hidden = (act * pre_up).astype(BF16).astype(F32)
            terms = (hidden * raw_grad).reshape(4 * capacity, units)
            high = terms.astype(BF16)
            low = (terms - high.astype(F32)).astype(BF16)
            ones = jnp.ones((8, units), BF16)
            lined = lax.dot_general(
                ones, high, (((1,), (1,)), ((), ())), preferred_element_type=F32
            ) + lax.dot_general(ones, low, (((1,), (1,)), ((), ())), preferred_element_type=F32)
            dots[pl.ds(k, 1), pl.ds(0, 4 * capacity)] = lined[:1]
            grads[k, :, pl.ds(0, units)] = (
                (raw_grad * pre_up * slope).reshape(4 * capacity, units).astype(BF16)
            )
            grads[k, :, pl.ds(units, units)] = (
                (raw_grad * act).reshape(4 * capacity, units).astype(BF16)
            )

        @pl.when(kind == BACK)
        def _():
            sides = []
            for side_index in range(2):
                start = pl.multiple_of(side_index * half + h * quarter, quarter)
                product = lax.dot_general(
                    grads[k],
                    both[pl.ds(start, quarter), :],
                    (((1,), (1,)), ((), ())),
                    preferred_element_type=F32,
                )
                sides.append(product.reshape(4, capacity, quarter))
            value = jnp.concatenate(sides, axis=1).astype(BF16)
            for one in range(4):
                part[c, one % 2, one // 2] = value[one]
            part_to_mate(c).start()

        @pl.when(kind == SUM)
        def _():
            part_to_mate(c).wait_recv()
            total = part[c, core, 1 - row].astype(F32) + mate_in[c, 1 - row].astype(F32)
            mid[c] = total.astype(BF16)
            sum_to_cross(c).start()

        @pl.when(kind == FINISH)
        def _():
            sum_to_cross(c).wait_recv()
            total = part[c, core, row].astype(F32) + mate_in[c, row].astype(F32)
            total = (total + cross_in[c].astype(F32)).astype(BF16)

            @pl.when(k == 0)
            def _():
                landing[h, ctx] = total

            @pl.when(k > 0)
            def _():
                done[c] = total
                give_back(k, h).start()

        @pl.when(kind == DOTS)
        def _():
            for q in range(3):
                dots_to(q).start()

        @pl.when(kind == TOTALS)
        def _():
            for q in range(3):
                dots_to(q).wait_recv()
            dots_sum[...] = dots[...] + dots_in[0] + dots_in[1] + dots_in[2]

            @pl.loop(1, count)
            def _(k):
                totals_to(k).start()

    dots_all[pl.ds(ctx, 1), :] = dots_sum[:1]

    @pl.loop(1, count)
    def _(k):
        totals_to(k).wait()
        dots_all[pl.ds(partner(k), 1), :] = dots_back[k, pl.ds(k, 1), :]

    at = lax.broadcasted_iota(jnp.int32, (LANES, tokens), 0)
    here = (at == routed[pl.ds(0, 1), :] + exp * capacity).astype(BF16)
    gathered = jnp.zeros((count, tokens), F32)
    rest = dots_all[...]
    for _ in range(3):
        high = rest.astype(BF16)
        rest = rest - high.astype(F32)
        gathered = gathered + jnp.dot(high, here, preferred_element_type=F32)
    labels = lax.broadcasted_iota(jnp.int32, (count, tokens), 0)
    gate_grad = jnp.sum(
        jnp.where(ids[pl.ds(0, 1), :] == labels, gathered, 0.0), axis=0, keepdims=True
    )
    probability = stats[pl.ds(0, 8), :]
    prob_grad = gate_grad * stats[pl.ds(8, 8), :]
    logit_grad = probability * (
        prob_grad - jnp.sum(probability * prob_grad, axis=0, keepdims=True)
    )
    high = logit_grad.astype(BF16).astype(F32)
    middle = (logit_grad - high).astype(BF16).astype(F32)
    low = logit_grad - high - middle
    lines = jnp.concatenate(
        [high, middle, low, jnp.zeros((LANES - 24, tokens), F32)], axis=0
    )
    logit_lines = lines.T.astype(BF16)
    gate = turned[:, pl.ds(0, 1)]
    place = turned[:, pl.ds(8, 1)].astype(jnp.int32)
    spot = lax.broadcasted_iota(jnp.int32, (tokens, 2 * capacity * count), 1)
    thrice = jnp.concatenate(
        [router[...].astype(F32)] * 3 + [jnp.zeros((LANES - 24, width), F32)], axis=0
    ).astype(BF16)
    total[...] = jnp.zeros_like(total)
    for h in range(2):

        @pl.loop(1, count)
        def _(k):
            give_back(k, h).wait_recv()

        found = landing[h].reshape(2 * capacity * count, quarter)
        for half_index in range(2):
            start = half_index * half + h * quarter
            columns = pl.ds(start, quarter)
            own = (place + half_index * capacity == spot).astype(BF16)
            back = gate * jnp.dot(own, found, preferred_element_type=F32)
            back = back + jnp.dot(
                logit_lines, thrice[:, start : start + quarter], preferred_element_type=F32
            )
            back = back * gain[:, columns]
            acc[2 * half_index + h, :, pl.ds(0, quarter)] = back
            along = back * hidden[:, columns].astype(F32)
            some = along[:, :LANES]
            for one in range(1, quarter // LANES):
                some = some + along[:, one * LANES : (one + 1) * LANES]
            total[...] += some

    @pl.loop(0, tokens // 32)
    def _(i):
        some = pl.ds(pl.multiple_of(i * 32, 32), 32)
        factor = inverse[some, pl.ds(0, 1)]
        weight = jnp.sum(total[some, :], axis=1, keepdims=True) * factor**3 / width
        for block in range(4):
            columns = pl.ds(block * quarter, quarter)
            out_ref[some, columns] = (
                factor * acc[block, some, pl.ds(0, quarter)]
                - hidden[some, columns].astype(F32) * weight
            ).astype(BF16)

    for q in range(3):
        dots_to(q).wait_send()

    @pl.loop(0, 2 * count)
    def _(c):
        k, h = lax.div(c, 2), lax.rem(c, 2)
        to_mate(k, h).wait_send()
        to_cross(k, h).wait_send()
        relay(k, h).wait_send()
        part_to_mate(c).wait_send()
        sum_to_cross(c).wait_send()

        @pl.when(k > 0)
        def _():
            direct(k, h).wait_send()
            give_back(k, h).wait_send()


def exchange_kernel(capacity, hidden_states, upstream, gain, router, ids, w_gate, w_up, w_down):
    tokens, width = hidden_states.shape
    count, tall = router.shape[0], 2 * capacity
    units = w_down.shape[1]
    quarter = width // 4
    pieces = 2 * count
    rows_up = 4 * (-(-capacity // 16) * 16)
    hbm = pl.BlockSpec(memory_space=pl.ANY)
    return pl.pallas_call(
        functools.partial(exchange_body, count, capacity),
        out_shape=jax.ShapeDtypeStruct((tokens, width), BF16),
        in_specs=[hbm] * 8,
        out_specs=pl.BlockSpec(memory_space=pltpu.VMEM),
        scratch_shapes=[
            pltpu.VMEM((tokens, width), BF16),
            pltpu.VMEM((2 * tokens, width), BF16),
            pltpu.VMEM((1, width), F32),
            pltpu.VMEM((count, width), BF16),
            pltpu.VMEM(ids.shape, jnp.int32),
            pltpu.VMEM((tokens, LANES), F32),
            pltpu.VMEM((8, tokens), jnp.int32),
            pltpu.VMEM((16, tokens), F32),
            pltpu.VMEM((tokens, LANES), F32),
            pltpu.VMEM((count, tall, width), BF16),
            pltpu.VMEM((2, count, tall, quarter), BF16),
            pltpu.VMEM((width, 2 * units), BF16),
            pltpu.VMEM((units, width), BF16),
            pltpu.VMEM((count, 4, tall, width), BF16),
            pltpu.VMEM((count, rows_up, 3 * units), F32),
            pltpu.VMEM((count, 4 * capacity, 2 * units), BF16),
            pltpu.VMEM((pieces, 2, 2, tall, quarter), BF16),
            pltpu.VMEM((pieces, 2, tall, quarter), BF16),
            pltpu.VMEM((pieces, tall, quarter), BF16),
            pltpu.VMEM((pieces, tall, quarter), BF16),
            pltpu.VMEM((pieces, tall, quarter), BF16),
            pltpu.VMEM((count, LANES), F32),
            pltpu.VMEM((3, count, LANES), F32),
            pltpu.VMEM((count, LANES), F32),
            pltpu.VMEM((count, count, LANES), F32),
            pltpu.VMEM((count, LANES), F32),
            pltpu.VMEM((tokens, LANES), F32),
            pltpu.SemaphoreType.DMA((3,)),
            pltpu.SemaphoreType.DMA((4 + tokens // 32,)),
            pltpu.SemaphoreType.DMA((7, pieces)),
            pltpu.SemaphoreType.DMA((7, pieces)),
            pltpu.SemaphoreType.DMA((2 + count,)),
            pltpu.SemaphoreType.DMA((2 + count,)),
        ],
        compiler_params=pltpu.CompilerParams(
            collective_id=0, has_side_effects=True, vmem_limit_bytes=52 * 2**20
        ),
    )(
        *(
            pltpu.with_memory_space_constraint(one, pltpu.HBM)
            for one in (hidden_states, upstream, gain, router, ids, w_gate, w_up, w_down)
        )
    )


def per_device(hidden_states, upstream, norm_gain, router, expert_ids, w_gate, w_up, w_down):
    tok_rows, model_width = hidden_states.shape
    experts = router.shape[1]
    capacity = 3 * tok_rows // (2 * experts)
    slot_total = experts * capacity
    if (
        capacity == 24 and experts == 8 and lax.axis_size("exp") == 4 and tok_rows == LANES
        and model_width % 1024 == 0
    ):
        return exchange_kernel(
            capacity, hidden_states, upstream, norm_gain[None, :], router.T, expert_ids.T,
            w_gate, w_up, w_down,
        )
    labels = jnp.arange(experts, dtype=jnp.int32)
    chosen = (expert_ids[:, :, None] == labels).astype(F32)
    primary = chosen[:, 0, :]
    member = jnp.sum(chosen, axis=1)
    lower = (
        jnp.arange(tok_rows)[:, None] > jnp.arange(tok_rows)[None, :]
    ).astype(BF16)
    before = jnp.dot(lower, primary.astype(BF16), preferred_element_type=F32)
    slot_index = jnp.sum(before * primary, axis=1).astype(jnp.int32)
    target = expert_ids[:, 0] * capacity + slot_index

    widened = hidden_states.astype(F32)
    inverse = lax.rsqrt(jnp.mean(widened * widened, axis=1, keepdims=True) + EPSILON)
    normed = (widened * inverse * norm_gain).astype(BF16)

    slots_up = pick(target, slot_total, upstream).reshape(experts, capacity, model_width)
    slots_normed = pick(target, slot_total, normed).reshape(experts, capacity, model_width)
    returned, dots = exchange_collective(
        slots_normed, slots_up, w_gate[0], w_up[0], w_down[0]
    )
    own = target[:, None] == jnp.arange(slot_total, dtype=jnp.int32)[None, :]
    raw_back = jnp.dot(own.astype(BF16), returned, preferred_element_type=F32)
    gate_grad = jnp.sum(jnp.where(own, dots[None, :], 0.0), axis=1)

    logits = jnp.dot(normed, router, preferred_element_type=F32)
    probability = jax.nn.softmax(logits, axis=1)
    top_prob = jnp.sum(probability * primary, axis=1)
    route_mass = jnp.sum(probability * member, axis=1)
    gate_value = top_prob / route_mass

    expert_grad = gate_value[:, None] * raw_back
    prob_grad = gate_grad[:, None] * (
        primary / route_mass[:, None] - (top_prob / (route_mass * route_mass))[:, None] * member
    )
    logit_grad = probability * (prob_grad - jnp.sum(probability * prob_grad, axis=1, keepdims=True))
    normed_grad = expert_grad + jnp.dot(
        logit_grad, router.astype(F32).T, precision=lax.Precision.HIGHEST
    )
    scaled = normed_grad * norm_gain
    grad_input = (
        inverse * scaled
        - widened * inverse**3 * jnp.sum(scaled * widened, axis=1, keepdims=True) / model_width
    )
    return grad_input.astype(BF16)


def solution(mesh):
    placed = (
        P(("ctx", "exp"), None),
        P(("ctx", "exp"), None),
        P(),
        P(),
        P(("ctx", "exp"), None),
        P("ctx", None, "exp"),
        P("ctx", None, "exp"),
        P("ctx", "exp", None),
    )
    return jax.shard_map(
        per_device, mesh=mesh, in_specs=placed, out_specs=P(("ctx", "exp"), None), check_vma=False
    )
```
